128 devices in a mesh: grp: 8 (over y_lo, z), wide: 16 (over y_hi, x, core).
Axes of the slice: x: 4, y: 4 (y_hi: 2, y_lo: 2; y = y_hi * 2 + y_lo), z: 4, core: 2. Of those that a mesh axis runs over, the one named last changes fastest.
Arguments:
- half_integrals: bfloat16 [16, 8, 1024, 2048], P('wide', None, None, 'grp'), may hold values from -0.47851562 to 0.47851562
- coeff_virtual: bfloat16 [1024, 768], replicated, may hold values from -0.1875 to 0.1875
- occ_energy: float32 [16, 8], replicated, may hold values from -2 to -0.3
- vir_energy: float32 [768], replicated, may hold values from 0.2 to 3
- plan: int32 [2, 2], replicated, may hold values from 0 to 15, as said below
Outputs:
- density_three: float32 [16, 8, 768, 2048], P('wide', 'grp')
The draws below stay inside these ranges and needn't reach their ends.
Inputs may be any that keep to these rules, and one draw needn't show every extreme that they name: plan[s, k] is the owner block whose orbitals serve step s, slot k; the value 0 and the value 16 - 1 both occur in every draw, an owner may repeat.
All inputs are finite; a program needn't handle non-finite values.
Results may differ from the reference program's by a relative error of at most 0.0039.
Values may be sent and summed in bfloat16 or wider, within the bound.
No kernel may reach another device: no remote copies, remote signals or barrier semaphores. Data moves between devices by JAX's collectives and lax.ppermute only.
A program may use at most 128 MiB of HBM per device.

```python
import jax
import jax.numpy as jnp
from jax import lax

VIRT = 768
BASIS = 1024
AUX = 2048
STEPS = 2
NBLK = 16
OW = 8
N_GRP = 8


def draw_plan(key, part):
    others = jax.random.randint(jax.random.fold_in(key, 11), (2 * STEPS - 2,), 1, NBLK - 1)
    values = jnp.concatenate([jnp.array([0, NBLK - 1], jnp.int32), others.astype(jnp.int32)])
    order = jax.random.permutation(jax.random.fold_in(key, 23), 2 * STEPS)
    return values[order].reshape(STEPS, 2).astype(jnp.int32)


def block_levels(stream_key, extent, pieces, smallest, largest):
    def one(dim, blocks):
        heights = jax.random.uniform(jax.random.fold_in(jax.random.fold_in(stream_key, 6), dim), (blocks,), jnp.float32, smallest / len(pieces), largest / len(pieces))
        return jnp.repeat(jnp.exp(heights), extent[dim] // blocks).reshape((-1,) + (1,) * (len(extent) - dim - 1))

    loudness = one(*pieces[0])
    for cut in pieces[1:]:
        loudness = loudness * one(*cut)
    return loudness


def normal_values(own_key, shape, scale, most, pieces=(), held_as=jnp.bfloat16):
    values = jax.random.normal(own_key, shape, jnp.float32) * scale
    if len(pieces) > 0:
        values = block_levels(own_key, shape, pieces, -0.22, 0.18) * values
    return jnp.clip(values, min=-most, max=most).astype(held_as)


def setup_inputs(seed: int = 0) -> dict:
    keys = jax.random.split(jax.random.key(seed), 6)
    half_integrals = normal_values(keys[0], (NBLK, OW, BASIS, AUX), 0.08, 0.47851562, ((0, 16), (3, 8)))
    coeff_virtual = normal_values(keys[1], (BASIS, VIRT), BASIS ** -0.5, 0.1875)
    occ_energy = jnp.clip(jax.random.uniform(keys[2], (NBLK, OW), jnp.float32, -2.0, -0.3), -2.0, -0.3)
    vir_energy = jnp.clip(jax.random.uniform(keys[3], (VIRT,), jnp.float32, 0.2, 3.0), 0.2, 3.0)
    plan = draw_plan(jax.random.fold_in(keys[5], 71), 0)
    return dict(half_integrals=half_integrals, coeff_virtual=coeff_virtual, occ_energy=occ_energy, vir_energy=vir_energy, plan=plan)


def pair_terms(rows_i, rows_j, energy_i, energy_j, vir_energy):
    left = rows_i.astype(jnp.float32)
    right = rows_j.astype(jnp.float32)
    intersection = jnp.einsum("iap,jbp->ijab", left, right)
    denominator = (energy_i[:, None, None, None] + energy_j[None, :, None, None]
                   - vir_energy[None, None, :, None] - vir_energy[None, None, None, :])
    amplitude = intersection / denominator
    combined = (2.0 * amplitude - jnp.swapaxes(amplitude, 2, 3)).astype(jnp.bfloat16)
    return jnp.einsum("ijab,jbp->iap", combined.astype(jnp.float32), right)


def reference(half_integrals, coeff_virtual, occ_energy, vir_energy, plan):
    coeff_wide = coeff_virtual.astype(jnp.float32)

    def transform(block):
        return jnp.einsum("imp,ma->iap", block.astype(jnp.float32), coeff_wide).astype(jnp.bfloat16)

    rows_all = lax.map(transform, half_integrals)
    per_dev = OW // N_GRP
    grouped = rows_all.reshape(NBLK, N_GRP, per_dev, VIRT, AUX)
    energies = occ_energy.reshape(NBLK, N_GRP, per_dev)

    def one_group(flat_index):
        block_index = flat_index // N_GRP
        group_index = flat_index % N_GRP
        rows_i = grouped[block_index, group_index]
        energy_i = energies[block_index, group_index]
        total = jnp.zeros((per_dev, VIRT, AUX), jnp.float32)
        for step_index in range(STEPS):
            for slot_index in range(2):
                owner_index = plan[step_index, slot_index]
                rows_j = grouped[owner_index, group_index]
                energy_j = energies[owner_index, group_index]
                total = total + pair_terms(rows_i, rows_j, energy_i, energy_j, vir_energy)
        return total

    result = lax.map(one_group, jnp.arange(NBLK * N_GRP, dtype=jnp.int32))
    return result.reshape(NBLK, OW, VIRT, AUX)
```

```python
import jax
import jax.numpy as jnp
from jax import lax
from jax.experimental import pallas as pl
from jax.experimental.pallas import tpu as pltpu
from jax.sharding import Mesh, PartitionSpec as P

GRP = ("ylo", "z")
WIDE = ("yhi", "x", "core")
ALL = GRP + WIDE
NWIDE = 16
NGRP = 8


def swap(value, axis):
    return lax.ppermute(value, axis, [(0, 1), (1, 0)])


def shift(value, step):
    return lax.ppermute(value, "x", [(i, (i + step) % 4) for i in range(4)])


def gather_wide(own):
    other = swap(own, "yhi")
    own_r, own_l = shift(own, 1), shift(own, -1)
    oth_r, oth_l = shift(other, 1), shift(other, -1)
    own_far, oth_far = shift(own_r, 1), shift(oth_l, -1)
    mine = [own, other, own_r, own_l, oth_r, oth_l, own_far, oth_far]
    return mine + [swap(block, "core") for block in mine]


def block_indices():
    yhi, x, core = (lax.axis_index(a) for a in WIDE)
    places = [(0, 0), (1, 0), (0, 3), (0, 1), (1, 3), (1, 1), (0, 2), (1, 2)]
    out = []
    for flip in (0, 1):
        for dy, dx in places:
            out.append(((yhi ^ dy) * 4 + (x + dx) % 4) * 2 + (core ^ flip))
    return jnp.stack(out).astype(jnp.int32)


def pair_kernel(count, has_acc, *refs):
    where_ref, energy_ref, vcol_ref, vrow_ref, rows_i_ref = refs[:5]
    blocks = refs[5:5 + NWIDE]
    refs = refs[5 + NWIDE:]
    if has_acc:
        acc_ref, refs = refs[0], refs[1:]
    out_ref, rows_i, rows_j, amp, comb, obuf, abuf, in_sem, out_sem, acc_sem = refs
    virt, aux = rows_i.shape
    part = blocks[0].shape[1]
    wide_p = rows_i_ref.shape[2]
    step = obuf.shape[2]
    nstep = aux // step
    copies = []
    for g in range(NGRP):
        copies.append(pltpu.make_async_copy(
            rows_i_ref.at[g], rows_i.at[:, pl.ds(g * wide_p, wide_p)], in_sem))
    for k in range(count):
        for b in range(NWIDE):
            start = pl.multiple_of(where_ref[b] * part, 16)
            copies.append(pltpu.make_async_copy(
                blocks[b].at[k], rows_j.at[pl.ds(k * virt + start, part), :], in_sem))
    for c in copies:
        c.start()

    def acc_copy(n):
        return pltpu.make_async_copy(
            acc_ref.at[:, pl.ds(n * step, step)], abuf.at[n % 2], acc_sem.at[n % 2])

    def out_copy(n):
        return pltpu.make_async_copy(
            obuf.at[n % 2], out_ref.at[:, pl.ds(n * step, step)], out_sem.at[n % 2])

    if has_acc:
        acc_copy(0).start()
    for c in copies:
        c.wait()
    tile = 256
    for k in range(count):
        inter = lax.dot_general(
            rows_i[...], rows_j[k * virt:(k + 1) * virt, :], (((1,), (1,)), ((), ())),
            preferred_element_type=jnp.float32)
        denom = (energy_ref[0] + energy_ref[1 + k]) - vcol_ref[...] - vrow_ref[...]
        amp[...] = inter / denom
        for i in range(virt // tile):
            for j in range(virt // tile):
                here = amp[i * tile:(i + 1) * tile, j * tile:(j + 1) * tile]
                there = amp[j * tile:(j + 1) * tile, i * tile:(i + 1) * tile]
                comb[i * tile:(i + 1) * tile, k * virt + j * tile:k * virt + (j + 1) * tile] = (
                    2.0 * here - there.T).astype(jnp.bfloat16)
    for n in range(nstep):
        if has_acc and n + 1 < nstep:
            acc_copy(n + 1).start()
        total = jnp.dot(comb[...], rows_j[:, n * step:(n + 1) * step],
                        preferred_element_type=jnp.float32)
        if has_acc:
            acc_copy(n).wait()
            total = total + abuf[n % 2]
        if n >= 2:
            out_copy(n - 2).wait()
        obuf[n % 2] = total
        out_copy(n).start()
    for n in range(max(nstep - 2, 0), nstep):
        out_copy(n).wait()


def pair_terms(where, energies, vir, rows_i, blocks, acc):
    count, part, aux = blocks[0].shape
    virt = rows_i.shape[1]
    step = 512
    anyspec = pl.BlockSpec(memory_space=pl.ANY)
    smem = pl.BlockSpec(memory_space=pltpu.SMEM)
    vmem = pl.BlockSpec(memory_space=pltpu.VMEM)
    args = [where, energies, vir[:, None], vir[None, :], rows_i, *blocks]
    specs = [smem, smem, vmem, vmem] + [anyspec] * (1 + NWIDE)
    if acc is not None:
        args.append(acc)
        specs.append(anyspec)

    def body(*refs):
        pair_kernel(count, acc is not None, *refs)

    return pl.pallas_call(
        body,
        out_shape=jax.ShapeDtypeStruct((virt, aux), jnp.float32),
        in_specs=specs,
        out_specs=anyspec,
        scratch_shapes=[
            pltpu.VMEM((virt, aux), jnp.bfloat16),
            pltpu.VMEM((count * virt, aux), jnp.bfloat16),
            pltpu.VMEM((virt, virt), jnp.float32),
            pltpu.VMEM((virt, count * virt), jnp.bfloat16),
            pltpu.VMEM((2, virt, step), jnp.float32),
            pltpu.VMEM((2, virt, step), jnp.float32),
            pltpu.SemaphoreType.DMA,
            pltpu.SemaphoreType.DMA((2,)),
            pltpu.SemaphoreType.DMA((2,)),
        ],
        compiler_params=pltpu.CompilerParams(vmem_limit_bytes=56 * 1024 * 1024),
        cost_estimate=pl.CostEstimate(
            flops=4 * count * virt * virt * aux, transcendentals=0,
            bytes_accessed=2 * (count + 1) * virt * aux + 4 * virt * aux),
        name="pair_terms",
    )(*args)


def shards(half_integrals, coeff_virtual, occ_energy, vir_energy, plan):
    rows = jnp.einsum(
        "imp,ma->iap", half_integrals[0], coeff_virtual, preferred_element_type=jnp.float32
    ).astype(jnp.bfloat16)
    orbs, virt, cols = rows.shape
    part = virt // NWIDE
    spread = lax.all_to_all(rows.reshape(orbs * NWIDE, part, cols), ALL, 0, 0, tiled=True)
    spread = spread.reshape(NGRP, NWIDE, part, cols)
    owners = plan.reshape(-1)
    mine = [
        lax.dynamic_index_in_dim(spread, owners[k], 1, keepdims=False)
        .transpose(1, 0, 2).reshape(part, NGRP * cols)
        for k in range(4)
    ]
    first = gather_wide(jnp.stack(mine[:2]))
    second = gather_wide(jnp.stack(mine[2:]))
    rows_i = lax.all_to_all(rows, GRP, 0, 0, tiled=True)
    grp = lax.axis_index(GRP)
    wide = lax.axis_index(WIDE)
    energy = lax.dynamic_slice_in_dim(occ_energy, grp, 1, 1)[:, 0]
    my_energy = lax.dynamic_slice_in_dim(energy, wide, 1)
    where = block_indices()
    e_own = jnp.take(energy, owners, axis=0)
    density = pair_terms(where, jnp.concatenate([my_energy, e_own[:2]]), vir_energy,
                         rows_i, first, None)
    density = pair_terms(where, jnp.concatenate([my_energy, e_own[2:]]), vir_energy,
                         rows_i, second, density)
    return density[None, None]


def solution(mesh):
    fine = Mesh(mesh.devices.reshape(2, 4, 2, 4, 2), ALL)
    return jax.shard_map(
        shards,
        mesh=fine,
        in_specs=(P(WIDE, None, None, GRP), P(), P(), P(), P()),
        out_specs=P(WIDE, GRP, None, None),
        check_vma=False,
    )
```

```python
import jax
import jax.numpy as jnp
from jax import lax
from jax.experimental import pallas as pl
from jax.experimental.pallas import tpu as pltpu
from jax.sharding import Mesh, PartitionSpec as P

GRP = ("ylo", "z")
WIDE = ("yhi", "x", "core")
ALL = GRP + WIDE
NWIDE = 16
NGRP = 8


def swap(value, axis):
    return lax.ppermute(value, axis, [(0, 1), (1, 0)])


def shift(value, step):
    return lax.ppermute(value, "x", [(i, (i + step) % 4) for i in range(4)])


def gather_rounds(firsts, seconds, after_swap):
    tie = lax.optimization_barrier
    other1 = swap(firsts, "yhi")
    own1_r, own1_l = shift(firsts, 1), shift(firsts, -1)
    other2 = swap(seconds, "yhi")
    other1, own1_r, own1_l = tie((other1, own1_r, own1_l))
    oth1_r, oth1_l = shift(other1, 1), shift(other1, -1)
    own2_r, own2_l = shift(seconds, 1), shift(seconds, -1)
    other2, after_swap, other1 = tie((other2, after_swap, other1))
    oth1_r, oth1_l, own1_r = tie((oth1_r, oth1_l, own1_r))
    far1_own, far1_oth = shift(own1_r, 1), shift(oth1_l, -1)
    other2, own2_r, own2_l, far1_own, far1_oth = tie(
        (other2, own2_r, own2_l, far1_own, far1_oth))
    oth2_r, oth2_l = shift(other2, 1), shift(other2, -1)
    oth2_r, oth2_l, own2_r = tie((oth2_r, oth2_l, own2_r))
    far2_own, far2_oth = shift(own2_r, 1), shift(oth2_l, -1)
    mine1 = [firsts, other1, own1_r, own1_l, oth1_r, oth1_l, far1_own, far1_oth]
    mine2 = [seconds, other2, own2_r, own2_l, oth2_r, oth2_l, far2_own, far2_oth]
    return (mine1 + [swap(block, "core") for block in mine1],
            mine2 + [swap(block, "core") for block in mine2], after_swap)


def pick_kernel(plan_ref, spread_ref, out_a, out_b, sem):
    cols = spread_ref.shape[3]
    copies = []
    for k, out in ((0, out_a), (1, out_a), (2, out_b), (3, out_b)):
        owner = plan_ref[k // 2, k % 2]
        for g in range(NGRP):
            copies.append(pltpu.make_async_copy(
                spread_ref.at[g, owner], out.at[k % 2, :, pl.ds(g * cols, cols)], sem))
    for c in copies:
        c.start()
    for c in copies:
        c.wait()


def pick_owners(plan, spread):
    part, cols = spread.shape[2:]
    one = jax.ShapeDtypeStruct((2, part, NGRP * cols), spread.dtype)
    anyspec = pl.BlockSpec(memory_space=pl.ANY)
    return pl.pallas_call(
        pick_kernel,
        out_shape=(one, one),
        in_specs=[pl.BlockSpec(memory_space=pltpu.SMEM), anyspec],
        out_specs=(anyspec, anyspec),
        scratch_shapes=[pltpu.SemaphoreType.DMA],
        name="pick_owners",
    )(plan, spread)


def block_indices():
    yhi, x, core = (lax.axis_index(a) for a in WIDE)
    places = [(0, 0), (1, 0), (0, 3), (0, 1), (1, 3), (1, 1), (0, 2), (1, 2)]
    out = []
    for flip in (0, 1):
        for dy, dx in places:
            out.append(((yhi ^ dy) * 4 + (x + dx) % 4) * 2 + (core ^ flip))
    return jnp.stack(out).astype(jnp.int32)


def pair_kernel(count, has_acc, *refs):
    where_ref, energy_ref, vcol_ref, vrow_ref, rows_i_ref = refs[:5]
    blocks = refs[5:5 + NWIDE]
    refs = refs[5 + NWIDE:]
    if has_acc:
        acc_ref, refs = refs[0], refs[1:]
    out_ref, rows_i, rows_j, amp, comb, obuf, abuf, in_sem, out_sem, acc_sem = refs
    virt, aux = rows_i.shape
    part = blocks[0].shape[1]
    wide_p = rows_i_ref.shape[2]
    step = obuf.shape[2]
    nstep = aux // step
    copies = []
    for g in range(NGRP):
        copies.append(pltpu.make_async_copy(
            rows_i_ref.at[g], rows_i.at[:, pl.ds(g * wide_p, wide_p)], in_sem))
    for k in range(count):
        for b in range(NWIDE):
            start = pl.multiple_of(where_ref[b] * part, 16)
            copies.append(pltpu.make_async_copy(
                blocks[b].at[k], rows_j.at[pl.ds(k * virt + start, part), :], in_sem))
    for c in copies:
        c.start()

    def acc_copy(n):
        return pltpu.make_async_copy(
            acc_ref.at[:, pl.ds(n * step, step)], abuf.at[n % 2], acc_sem.at[n % 2])

    def out_copy(n):
        return pltpu.make_async_copy(
            obuf.at[n % 2], out_ref.at[:, pl.ds(n * step, step)], out_sem.at[n % 2])

    if has_acc:
        acc_copy(0).start()
    for c in copies:
        c.wait()
    tile = 256
    for k in range(count):
        inter = lax.dot_general(
            rows_i[...], rows_j[k * virt:(k + 1) * virt, :], (((1,), (1,)), ((), ())),
            preferred_element_type=jnp.float32)
        denom = (energy_ref[0] + energy_ref[1 + k]) - vcol_ref[...] - vrow_ref[...]
        amp[...] = inter / denom
        for i in range(virt // tile):
            for j in range(virt // tile):
                here = amp[i * tile:(i + 1) * tile, j * tile:(j + 1) * tile]
                there = amp[j * tile:(j + 1) * tile, i * tile:(i + 1) * tile]
                comb[i * tile:(i + 1) * tile, k * virt + j * tile:k * virt + (j + 1) * tile] = (
                    2.0 * here - there.T).astype(jnp.bfloat16)
    for n in range(nstep):
        if has_acc and n + 1 < nstep:
            acc_copy(n + 1).start()
        total = jnp.dot(comb[...], rows_j[:, n * step:(n + 1) * step],
                        preferred_element_type=jnp.float32)
        if has_acc:
            acc_copy(n).wait()
            total = total + abuf[n % 2]
        if n >= 2:
            out_copy(n - 2).wait()
        obuf[n % 2] = total
        out_copy(n).start()
    for n in range(max(nstep - 2, 0), nstep):
        out_copy(n).wait()


def pair_terms(where, energies, vcol, vrow, rows_i, blocks, acc):
    count, part, aux = blocks[0].shape
    virt = rows_i.shape[1]
    step = 512
    anyspec = pl.BlockSpec(memory_space=pl.ANY)
    smem = pl.BlockSpec(memory_space=pltpu.SMEM)
    vmem = pl.BlockSpec(memory_space=pltpu.VMEM)
    args = [where, energies, vcol, vrow, rows_i, *blocks]
    specs = [smem, smem, vmem, vmem] + [anyspec] * (1 + NWIDE)
    if acc is not None:
        args.append(acc)
        specs.append(anyspec)

    def body(*refs):
        pair_kernel(count, acc is not None, *refs)

    return pl.pallas_call(
        body,
        out_shape=jax.ShapeDtypeStruct((virt, aux), jnp.float32),
        in_specs=specs,
        out_specs=anyspec,
        scratch_shapes=[
            pltpu.VMEM((virt, aux), jnp.bfloat16),
            pltpu.VMEM((count * virt, aux), jnp.bfloat16),
            pltpu.VMEM((virt, virt), jnp.float32),
            pltpu.VMEM((virt, count * virt), jnp.bfloat16),
            pltpu.VMEM((2, virt, step), jnp.float32),
            pltpu.VMEM((2, virt, step), jnp.float32),
            pltpu.SemaphoreType.DMA,
            pltpu.SemaphoreType.DMA((2,)),
            pltpu.SemaphoreType.DMA((2,)),
        ],
        compiler_params=pltpu.CompilerParams(vmem_limit_bytes=56 * 1024 * 1024),
        cost_estimate=pl.CostEstimate(
            flops=4 * count * virt * virt * aux, transcendentals=0,
            bytes_accessed=2 * (count + 1) * virt * aux + 4 * virt * aux),
        name="pair_terms",
    )(*args)


def shards(half_integrals, coeff_virtual, occ_energy, vir_energy, plan):
    rows = jnp.einsum(
        "imp,ma->iap", half_integrals[0], coeff_virtual, preferred_element_type=jnp.float32
    ).astype(jnp.bfloat16)
    orbs, virt, cols = rows.shape
    part = virt // NWIDE
    spread = lax.all_to_all(rows.reshape(orbs * NWIDE, part, cols), ALL, 0, 0, tiled=True)
    spread = spread.reshape(NGRP, NWIDE, part, cols)
    owners = plan.reshape(-1)
    grp = lax.axis_index(GRP)
    wide = lax.axis_index(WIDE)
    energy = lax.dynamic_slice_in_dim(occ_energy, grp, 1, 1)[:, 0]
    my_energy = lax.dynamic_slice_in_dim(energy, wide, 1)
    e_own = jnp.take(energy, owners, axis=0)
    small = (block_indices(), jnp.concatenate([my_energy, e_own[:2]]),
             jnp.concatenate([my_energy, e_own[2:]]), vir_energy[:, None], vir_energy[None, :])
    spread, (where, e_first, e_second, vcol, vrow) = lax.optimization_barrier((spread, small))
    first, second = pick_owners(plan, spread)
    first, second, rows = gather_rounds(first, second, rows)
    rows_i = lax.all_to_all(rows, GRP, 0, 0, tiled=True)
    density = pair_terms(where, e_first, vcol, vrow, rows_i, first, None)
    density = pair_terms(where, e_second, vcol, vrow, rows_i, second, density)
    return density[None, None]


def solution(mesh):
    fine = Mesh(mesh.devices.reshape(2, 4, 2, 4, 2), ALL)
    return jax.shard_map(
        shards,
        mesh=fine,
        in_specs=(P(WIDE, None, None, GRP), P(), P(), P(), P()),
        out_specs=P(WIDE, GRP, None, None),
        check_vma=False,
    )
```

```python
import jax
import jax.numpy as jnp
from jax import lax
from jax.experimental import pallas as pl
from jax.experimental.pallas import tpu as pltpu
from jax.sharding import Mesh, PartitionSpec as P

GRP = ("ylo", "z")
WIDE = ("yhi", "x", "core")
ALL = GRP + WIDE
NWIDE = 16
NGRP = 8


def swap(value, axis):
    return lax.ppermute(value, axis, [(0, 1), (1, 0)])


def shift(value, step):
    return lax.ppermute(value, "x", [(i, (i + step) % 4) for i in range(4)])


def gather_wide(own, after_swap):
    other = swap(own, "yhi")
    own_r, own_l = shift(own, 1), shift(own, -1)
    other, own_r, own_l, own, after_swap = lax.optimization_barrier(
        (other, own_r, own_l, own, after_swap))
    oth_r, oth_l = shift(other, 1), shift(other, -1)
    own_far, oth_far = shift(own, 2), shift(other, 2)
    mine = [own, other, own_r, own_l, oth_r, oth_l, own_far, oth_far]
    return mine + [swap(block, "core") for block in mine], after_swap


def pick_kernel(plan_ref, spread_ref, out_ref, sem):
    cols = spread_ref.shape[3]
    copies = []
    for k in range(4):
        owner = plan_ref[k // 2, k % 2]
        for g in range(NGRP):
            copies.append(pltpu.make_async_copy(
                spread_ref.at[g, owner], out_ref.at[k, :, pl.ds(g * cols, cols)], sem))
    for c in copies:
        c.start()
    for c in copies:
        c.wait()


def pick_owners(plan, spread):
    part, cols = spread.shape[2:]
    return pl.pallas_call(
        pick_kernel,
        out_shape=jax.ShapeDtypeStruct((4, part, NGRP * cols), spread.dtype),
        in_specs=[pl.BlockSpec(memory_space=pltpu.SMEM), pl.BlockSpec(memory_space=pl.ANY)],
        out_specs=pl.BlockSpec(memory_space=pltpu.VMEM),
        scratch_shapes=[pltpu.SemaphoreType.DMA],
        name="pick_owners",
    )(plan, spread)


def block_indices():
    yhi, x, core = (lax.axis_index(a) for a in WIDE)
    places = [(0, 0), (1, 0), (0, 3), (0, 1), (1, 3), (1, 1), (0, 2), (1, 2)]
    out = []
    for flip in (0, 1):
        for dy, dx in places:
            out.append(((yhi ^ dy) * 4 + (x + dx) % 4) * 2 + (core ^ flip))
    return jnp.stack(out).astype(jnp.int32)


def pair_kernel(count, *refs):
    where_ref, energy_ref, vir_ref, rows_i_ref = refs[:4]
    blocks = refs[4:4 + NWIDE]
    out_ref, rows_i, rows_j, amp, comb, obuf, in_sem, out_sem = refs[4 + NWIDE:]
    virt, aux = rows_i.shape
    part = blocks[0].shape[1]
    wide_p = rows_i_ref.shape[2]
    step = obuf.shape[2]
    nstep = aux // step
    copies = [[] for _ in range(count)]
    for g in range(NGRP):
        copies[0].append(pltpu.make_async_copy(
            rows_i_ref.at[g], rows_i.at[:, pl.ds(g * wide_p, wide_p)], in_sem.at[0]))
    for k in range(count):
        for b in range(NWIDE):
            start = pl.multiple_of(where_ref[b] * part, 16)
            copies[k].append(pltpu.make_async_copy(
                blocks[b].at[k], rows_j.at[pl.ds(k * virt + start, part), :], in_sem.at[k]))
    for group in copies:
        for c in group:
            c.start()

    def out_copy(n):
        return pltpu.make_async_copy(
            obuf.at[n % 2], out_ref.at[:, pl.ds(n * step, step)], out_sem.at[n % 2])

    vrow = vir_ref[...]
    vcol = jnp.broadcast_to(vrow, (128, virt)).T[:, :1]
    tile = 256
    for k in range(count):
        for c in copies[k]:
            c.wait()
        inter = lax.dot_general(
            rows_i[...], rows_j[k * virt:(k + 1) * virt, :], (((1,), (1,)), ((), ())),
            preferred_element_type=jnp.float32)
        amp[...] = inter / ((energy_ref[0] + energy_ref[1 + k]) - vcol - vrow)
        for i in range(virt // tile):
            for j in range(virt // tile):
                here = amp[i * tile:(i + 1) * tile, j * tile:(j + 1) * tile]
                there = amp[j * tile:(j + 1) * tile, i * tile:(i + 1) * tile]
                comb[i * tile:(i + 1) * tile, k * virt + j * tile:k * virt + (j + 1) * tile] = (
                    2.0 * here - there.T).astype(jnp.bfloat16)
    for n in range(nstep):
        total = jnp.dot(comb[...], rows_j[:, n * step:(n + 1) * step],
                        preferred_element_type=jnp.float32)
        if n >= 2:
            out_copy(n - 2).wait()
        obuf[n % 2] = total
        out_copy(n).start()
    for n in range(max(nstep - 2, 0), nstep):
        out_copy(n).wait()


def pair_terms(where, energies, vir, rows_i, blocks):
    count, part, aux = blocks[0].shape
    virt = rows_i.shape[1]
    step = 512
    anyspec = pl.BlockSpec(memory_space=pl.ANY)
    smem = pl.BlockSpec(memory_space=pltpu.SMEM)
    vmem = pl.BlockSpec(memory_space=pltpu.VMEM)

    def body(*refs):
        pair_kernel(count, *refs)

    return pl.pallas_call(
        body,
        out_shape=jax.ShapeDtypeStruct((virt, aux), jnp.float32),
        in_specs=[smem, smem, vmem] + [anyspec] * (1 + NWIDE),
        out_specs=anyspec,
        scratch_shapes=[
            pltpu.VMEM((virt, aux), jnp.bfloat16),
            pltpu.VMEM((count * virt, aux), jnp.bfloat16),
            pltpu.VMEM((virt, virt), jnp.float32),
            pltpu.VMEM((virt, count * virt), jnp.bfloat16),
            pltpu.VMEM((2, virt, step), jnp.float32),
            pltpu.SemaphoreType.DMA((count,)),
            pltpu.SemaphoreType.DMA((2,)),
        ],
        compiler_params=pltpu.CompilerParams(vmem_limit_bytes=56 * 1024 * 1024),
        cost_estimate=pl.CostEstimate(
            flops=4 * count * virt * virt * aux, transcendentals=0,
            bytes_accessed=2 * (count + 1) * virt * aux + 4 * virt * aux),
        name="pair_terms",
    )(where, energies, vir, rows_i, *blocks)


def shards(half_integrals, coeff_virtual, occ_energy, vir_energy, plan):
    rows = jnp.einsum(
        "imp,ma->iap", half_integrals[0], coeff_virtual, preferred_element_type=jnp.float32
    ).astype(jnp.bfloat16)
    orbs, virt, cols = rows.shape
    part = virt // NWIDE
    spread = lax.all_to_all(rows.reshape(orbs * NWIDE, part, cols), ALL, 0, 0, tiled=True)
    spread = spread.reshape(NGRP, NWIDE, part, cols)
    owners = plan.reshape(-1)
    grp = lax.axis_index(GRP)
    wide = lax.axis_index(WIDE)
    energy = lax.dynamic_slice_in_dim(occ_energy, grp, 1, 1)[:, 0]
    my_energy = lax.dynamic_slice_in_dim(energy, wide, 1)
    e_own = jnp.take(energy, owners, axis=0)
    small = (block_indices(), jnp.concatenate([my_energy, e_own]), vir_energy[None, :])
    spread, (where, energies, vrow) = lax.optimization_barrier((spread, small))
    blocks, rows = gather_wide(pick_owners(plan, spread), rows)
    rows_i = lax.all_to_all(rows, GRP, 0, 0, tiled=True)
    return pair_terms(where, energies, vrow, rows_i, blocks)[None, None]


def solution(mesh):
    fine = Mesh(mesh.devices.reshape(2, 4, 2, 4, 2), ALL)
    return jax.shard_map(
        shards,
        mesh=fine,
        in_specs=(P(WIDE, None, None, GRP), P(), P(), P(), P()),
        out_specs=P(WIDE, GRP, None, None),
        check_vma=False,
    )
```

```python
import jax
import jax.numpy as jnp
from jax import lax
from jax.experimental import pallas as pl
from jax.experimental.pallas import tpu as pltpu
from jax.sharding import Mesh, PartitionSpec as P


GRP = ("ylo", "z")
WIDE = ("yhi", "x", "core")
ALL = GRP + WIDE
NWIDE = 16
NGRP = 8


def swap(value, axis):
    return lax.ppermute(value, axis, [(0, 1), (1, 0)])


def shift(value, step):
    return lax.ppermute(value, "x", [(i, (i + step) % 4) for i in range(4)])


def gather_wide(own):
    other = swap(own, "yhi")
    own_r = shift(own, 1)
    own_l = shift(own, -1)
    other, own_r, own_l = lax.optimization_barrier((other, own_r, own_l))
    oth_l = shift(other, -1)
    oth_r = shift(other, 1)
    own_far = shift(own_r, 1)
    oth_far = shift(oth_l, -1)
    mine = [own, other, own_r, own_l, oth_r, oth_l, own_far, oth_far]
    return mine + [swap(block, "core") for block in mine]


def pick_kernel(plan_ref, spread_ref, out_ref, sem):
    cols = spread_ref.shape[3]
    copies = []
    for k in range(4):
        owner = plan_ref[k // 2, k % 2]
        for g in range(NGRP):
            copies.append(pltpu.make_async_copy(
                spread_ref.at[g, owner], out_ref.at[k, :, pl.ds(g * cols, cols)], sem))
    for c in copies:
        c.start()
    for c in copies:
        c.wait()


def pick_owners(plan, spread):
    part, cols = spread.shape[2:]
    return pl.pallas_call(
        pick_kernel,
        out_shape=jax.ShapeDtypeStruct((4, part, NGRP * cols), spread.dtype),
        in_specs=[pl.BlockSpec(memory_space=pltpu.SMEM), pl.BlockSpec(memory_space=pl.ANY)],
        out_specs=pl.BlockSpec(memory_space=pltpu.VMEM),
        scratch_shapes=[pltpu.SemaphoreType.DMA],
        name="pick_owners",
    )(plan, spread)


def block_indices():
    yhi, x, core = (lax.axis_index(a) for a in WIDE)
    places = [(0, 0), (1, 0), (0, 3), (0, 1), (1, 3), (1, 1), (0, 2), (1, 2)]
    out = []
    for flip in (0, 1):
        for dy, dx in places:
            out.append(((yhi ^ dy) * 4 + (x + dx) % 4) * 2 + (core ^ flip))
    return jnp.stack(out).astype(jnp.int32)


def pair_kernel(count, *refs):
    where_ref, energy_ref, vir_ref, rows_i_ref = refs[:4]
    blocks = refs[4:4 + NWIDE]
    out_ref, rows_i, rows_j, amp, comb, obuf, in_sem, out_sem = refs[4 + NWIDE:]
    virt, aux = rows_i.shape
    part = blocks[0].shape[1]
    wide_p = rows_i_ref.shape[2]
    step = obuf.shape[2]
    nstep = aux // step
    copies = [[] for _ in range(count)]
    for g in range(NGRP):
        copies[0].append(pltpu.make_async_copy(
            rows_i_ref.at[g], rows_i.at[:, pl.ds(g * wide_p, wide_p)], in_sem.at[0]))
    for k in range(count):
        for b in range(NWIDE):
            start = pl.multiple_of(where_ref[b] * part, 16)
            copies[k].append(pltpu.make_async_copy(
                blocks[b].at[k], rows_j.at[pl.ds(k * virt + start, part), :], in_sem.at[k]))
    for group in copies:
        for c in group:
            c.start()

    def out_copy(n):
        return pltpu.make_async_copy(
            obuf.at[n % 2], out_ref.at[:, pl.ds(n * step, step)], out_sem.at[n % 2])

    vrow = vir_ref[...]
    vcol = jnp.broadcast_to(vrow, (128, virt)).T[:, :1]
    tile = 256
    for k in range(count):
        for c in copies[k]:
            c.wait()
        inter = lax.dot_general(
            rows_i[...], rows_j[k * virt:(k + 1) * virt, :], (((1,), (1,)), ((), ())),
            preferred_element_type=jnp.float32)
        amp[...] = inter / ((energy_ref[0] + energy_ref[1 + k]) - vcol - vrow)
        for i in range(virt // tile):
            for j in range(virt // tile):
                here = amp[i * tile:(i + 1) * tile, j * tile:(j + 1) * tile]
                there = amp[j * tile:(j + 1) * tile, i * tile:(i + 1) * tile]
                comb[i * tile:(i + 1) * tile, k * virt + j * tile:k * virt + (j + 1) * tile] = (
                    2.0 * here - there.T).astype(jnp.bfloat16)
    for n in range(nstep):
        total = jnp.dot(comb[...], rows_j[:, n * step:(n + 1) * step],
                        preferred_element_type=jnp.float32)
        if n >= 2:
            out_copy(n - 2).wait()
        obuf[n % 2] = total
        out_copy(n).start()
    for n in range(max(nstep - 2, 0), nstep):
        out_copy(n).wait()


def pair_terms(where, energies, vir, rows_i, blocks):
    count, _, aux = blocks[0].shape
    virt = rows_i.shape[1]
    step = 512
    anyspec = pl.BlockSpec(memory_space=pl.ANY)
    smem = pl.BlockSpec(memory_space=pltpu.SMEM)
    vmem = pl.BlockSpec(memory_space=pltpu.VMEM)

    def body(*refs):
        pair_kernel(count, *refs)

    return pl.pallas_call(
        body,
        out_shape=jax.ShapeDtypeStruct((virt, aux), jnp.float32),
        in_specs=[smem, smem, vmem] + [anyspec] * (1 + NWIDE),
        out_specs=anyspec,
        scratch_shapes=[
            pltpu.VMEM((virt, aux), jnp.bfloat16),
            pltpu.VMEM((count * virt, aux), jnp.bfloat16),
            pltpu.VMEM((virt, virt), jnp.float32),
            pltpu.VMEM((virt, count * virt), jnp.bfloat16),
            pltpu.VMEM((2, virt, step), jnp.float32),
            pltpu.SemaphoreType.DMA((count,)),
            pltpu.SemaphoreType.DMA((2,)),
        ],
        compiler_params=pltpu.CompilerParams(vmem_limit_bytes=56 * 1024 * 1024),
        cost_estimate=pl.CostEstimate(
            flops=4 * count * virt * virt * aux, transcendentals=0,
            bytes_accessed=2 * (count + 1) * virt * aux + 4 * virt * aux),
        name="pair_terms",
    )(where, energies, vir, rows_i, *blocks)


def shards(half_integrals, coeff_virtual, occ_energy, vir_energy, plan):
    rows = jnp.einsum(
        "imp,ma->iap", half_integrals[0], coeff_virtual, preferred_element_type=jnp.float32
    ).astype(jnp.bfloat16)
    orbs, virt, cols = rows.shape
    part = virt // NWIDE
    spread = lax.all_to_all(rows.reshape(orbs * NWIDE, part, cols), ALL, 0, 0, tiled=True)
    spread = spread.reshape(NGRP, NWIDE, part, cols)
    owners = plan.reshape(-1)
    grp = lax.axis_index(GRP)
    wide = lax.axis_index(WIDE)
    energy = lax.dynamic_slice_in_dim(occ_energy, grp, 1, 1)[:, 0]
    my_energy = lax.dynamic_slice_in_dim(energy, wide, 1)
    e_own = jnp.take(energy, owners, axis=0)
    small = (block_indices(), jnp.concatenate([my_energy, e_own]), vir_energy[None, :])
    spread, (where, energies, vrow) = lax.optimization_barrier((spread, small))
    picked, rows = lax.optimization_barrier((pick_owners(plan, spread), rows))
    blocks = gather_wide(picked)
    rows_i = lax.all_to_all(rows, GRP, 0, 0, tiled=True)
    return pair_terms(where, energies, vrow, rows_i, blocks)[None, None]


def solution(mesh):
    fine = Mesh(mesh.devices.reshape(2, 4, 2, 4, 2), GRP + WIDE)
    return jax.shard_map(
        shards,
        mesh=fine,
        in_specs=(P(WIDE, None, None, GRP), P(), P(), P(), P()),
        out_specs=P(WIDE, GRP, None, None),
        check_vma=False,
    )
```

```python
import jax
import jax.numpy as jnp
from jax import lax
from jax.experimental import pallas as pl
from jax.experimental.pallas import tpu as pltpu
from jax.sharding import Mesh, PartitionSpec as P


GRP = ("ylo", "z")
WIDE = ("yhi", "x", "core")
ALL = GRP + WIDE
NWIDE = 16
NGRP = 8


def swap(value, axis):
    return lax.ppermute(value, axis, [(0, 1), (1, 0)])


def shift(value, step):
    return lax.ppermute(value, "x", [(i, (i + step) % 4) for i in range(4)])


def gather_wide(own):
    other = swap(own, "yhi")
    own_r = shift(own, 1)
    own_l = shift(own, -1)
    oth_l = shift(other, -1)
    oth_r = shift(other, 1)
    own_far = shift(own_r, 1)
    oth_far = shift(oth_l, -1)
    mine = [own, other, own_r, own_l, oth_r, oth_l, own_far, oth_far]
    out = list(mine)
    for block in mine:
        out.append(swap(block, "core"))
    return out


def pick_kernel(plan_ref, spread_ref, out_a, out_b, sem):
    cols = spread_ref.shape[3]
    copies = []
    for k in range(4):
        owner = plan_ref[k // 2, k % 2]
        out_ref = (out_a, out_b)[k // 2]
        for g in range(NGRP):
            copies.append(pltpu.make_async_copy(
                spread_ref.at[g, owner], out_ref.at[k % 2, :, pl.ds(g * cols, cols)], sem))
    for c in copies:
        c.start()
    for c in copies:
        c.wait()


def pick_owners(plan, spread):
    part, cols = spread.shape[2:]
    return pl.pallas_call(
        pick_kernel,
        out_shape=(jax.ShapeDtypeStruct((2, part, NGRP * cols), spread.dtype),) * 2,
        in_specs=[pl.BlockSpec(memory_space=pltpu.SMEM), pl.BlockSpec(memory_space=pl.ANY)],
        out_specs=(pl.BlockSpec(memory_space=pltpu.VMEM),) * 2,
        scratch_shapes=[pltpu.SemaphoreType.DMA],
        name="pick_owners",
    )(plan, spread)


def block_indices():
    yhi, x, core = (lax.axis_index(a) for a in WIDE)
    places = [(0, 0), (1, 0), (0, 3), (0, 1), (1, 3), (1, 1), (0, 2), (1, 2)]
    out = []
    for flip in (0, 1):
        for dy, dx in places:
            out.append(((yhi ^ dy) * 4 + (x + dx) % 4) * 2 + (core ^ flip))
    return jnp.stack(out).astype(jnp.int32)


def pair_kernel(count, has_acc, *refs):
    where_ref, energy_ref, vir_ref, rows_i_ref = refs[:4]
    blocks = refs[4:4 + NWIDE]
    refs = refs[4 + NWIDE:]
    if has_acc:
        acc_ref, refs = refs[0], refs[1:]
    out_ref, rows_i, rows_j, amp, comb, obuf, abuf, in_sem, out_sem, acc_sem = refs
    virt, aux = rows_i.shape
    part = blocks[0].shape[1]
    wide_p = rows_i_ref.shape[2]
    step = obuf.shape[2]
    nstep = aux // step
    copies = [[] for _ in range(count)]
    for g in range(NGRP):
        copies[0].append(pltpu.make_async_copy(
            rows_i_ref.at[g], rows_i.at[:, pl.ds(g * wide_p, wide_p)], in_sem.at[0]))
    for k in range(count):
        for b in range(NWIDE):
            start = pl.multiple_of(where_ref[b] * part, 16)
            copies[k].append(pltpu.make_async_copy(
                blocks[b].at[k], rows_j.at[pl.ds(k * virt + start, part), :], in_sem.at[k]))
    for group in copies:
        for c in group:
            c.start()

    def out_copy(n):
        return pltpu.make_async_copy(
            obuf.at[n % 2], out_ref.at[:, pl.ds(n * step, step)], out_sem.at[n % 2])

    def acc_copy(n):
        return pltpu.make_async_copy(
            acc_ref.at[:, pl.ds(n * step, step)], abuf.at[n % 2], acc_sem.at[n % 2])

    if has_acc:
        acc_copy(0).start()
    vrow = vir_ref[...]
    vcol = jnp.broadcast_to(vrow, (128, virt)).T[:, :1]
    tile = 256
    for k in range(count):
        for c in copies[k]:
            c.wait()
        inter = lax.dot_general(
            rows_i[...], rows_j[k * virt:(k + 1) * virt, :], (((1,), (1,)), ((), ())),
            preferred_element_type=jnp.float32)
        amp[...] = inter / ((energy_ref[0] + energy_ref[1 + k]) - vcol - vrow)
        for i in range(virt // tile):
            for j in range(virt // tile):
                here = amp[i * tile:(i + 1) * tile, j * tile:(j + 1) * tile]
                there = amp[j * tile:(j + 1) * tile, i * tile:(i + 1) * tile]
                comb[i * tile:(i + 1) * tile, k * virt + j * tile:k * virt + (j + 1) * tile] = (
                    2.0 * here - there.T).astype(jnp.bfloat16)
    for n in range(nstep):
        if has_acc and n + 1 < nstep:
            acc_copy(n + 1).start()
        total = jnp.dot(comb[...], rows_j[:, n * step:(n + 1) * step],
                        preferred_element_type=jnp.float32)
        if has_acc:
            acc_copy(n).wait()
            total = total + abuf[n % 2]
        if n >= 2:
            out_copy(n - 2).wait()
        obuf[n % 2] = total
        out_copy(n).start()
    for n in range(max(nstep - 2, 0), nstep):
        out_copy(n).wait()


def pair_terms(where, energies, vir, rows_i, blocks, acc):
    count, _, aux = blocks[0].shape
    virt = rows_i.shape[1]
    step = 512
    anyspec = pl.BlockSpec(memory_space=pl.ANY)
    smem = pl.BlockSpec(memory_space=pltpu.SMEM)
    vmem = pl.BlockSpec(memory_space=pltpu.VMEM)

    args = [where, energies, vir, rows_i, *blocks] + ([] if acc is None else [acc])

    def body(*refs):
        pair_kernel(count, acc is not None, *refs)

    return pl.pallas_call(
        body,
        out_shape=jax.ShapeDtypeStruct((virt, aux), jnp.float32),
        in_specs=[smem, smem, vmem] + [anyspec] * (len(args) - 3),
        out_specs=anyspec,
        scratch_shapes=[
            pltpu.VMEM((virt, aux), jnp.bfloat16),
            pltpu.VMEM((count * virt, aux), jnp.bfloat16),
            pltpu.VMEM((virt, virt), jnp.float32),
            pltpu.VMEM((virt, count * virt), jnp.bfloat16),
            pltpu.VMEM((2, virt, step), jnp.float32),
            pltpu.VMEM((2, virt, step), jnp.float32),
            pltpu.SemaphoreType.DMA((count,)),
            pltpu.SemaphoreType.DMA((2,)),
            pltpu.SemaphoreType.DMA((2,)),
        ],
        compiler_params=pltpu.CompilerParams(vmem_limit_bytes=56 * 1024 * 1024),
        cost_estimate=pl.CostEstimate(
            flops=4 * count * virt * virt * aux, transcendentals=0,
            bytes_accessed=2 * (count + 1) * virt * aux + 4 * virt * aux),
    )(*args)


def shards(half_integrals, coeff_virtual, occ_energy, vir_energy, plan):
    rows = jnp.einsum(
        "imp,ma->iap", half_integrals[0], coeff_virtual, preferred_element_type=jnp.float32
    ).astype(jnp.bfloat16)
    orbs, virt, cols = rows.shape
    part = virt // NWIDE
    spread = lax.all_to_all(rows.reshape(orbs * NWIDE, part, cols), ALL, 0, 0, tiled=True)
    spread = spread.reshape(NGRP, NWIDE, part, cols)
    owners = plan.reshape(-1)
    grp = lax.axis_index(GRP)
    wide = lax.axis_index(WIDE)
    energy = lax.dynamic_slice_in_dim(occ_energy, grp, 1, 1)[:, 0]
    my_energy = lax.dynamic_slice_in_dim(energy, wide, 1)
    e_own = jnp.take(energy, owners, axis=0)
    small = (block_indices(), jnp.concatenate([my_energy, e_own[:2]]),
             jnp.concatenate([my_energy, e_own[2:]]), vir_energy[None, :])
    spread, (where, e_first, e_second, vrow) = lax.optimization_barrier((spread, small))
    (first, second), rows = lax.optimization_barrier((pick_owners(plan, spread), rows))
    first = gather_wide(first)
    second = gather_wide(second)
    rows_i = lax.all_to_all(rows, GRP, 0, 0, tiled=True)
    density = pair_terms(where, e_first, vrow, rows_i, first, None)
    density = pair_terms(where, e_second, vrow, rows_i, second, density)
    return density[None, None]


def solution(mesh):
    fine = Mesh(mesh.devices.reshape(2, 4, 2, 4, 2), GRP + WIDE)
    return jax.shard_map(
        shards,
        mesh=fine,
        in_specs=(P(WIDE, None, None, GRP), P(), P(), P(), P()),
        out_specs=P(WIDE, GRP, None, None),
        check_vma=False,
    )
```

```python
import jax
import jax.numpy as jnp
from jax import lax
from jax.experimental import pallas as pl
from jax.experimental.pallas import tpu as pltpu
from jax.sharding import Mesh, PartitionSpec as P


GRP = ("ylo", "z")
WIDE = ("yhi", "x", "core")
ALL = GRP + WIDE
NWIDE = 16
NGRP = 8


def swap(value, axis):
    return lax.ppermute(value, axis, [(0, 1), (1, 0)])


def shift(value, step):
    return lax.ppermute(value, "x", [(i, (i + step) % 4) for i in range(4)])


def gather_wide(own):
    other = swap(own, "yhi")
    own_r = shift(own, 1)
    own_l = shift(own, -1)
    oth_l = shift(other, -1)
    oth_r = shift(other, 1)
    own_far = shift(own_r, 1)
    oth_far = shift(oth_l, -1)
    mine = [own, other, own_r, own_l, oth_r, oth_l, own_far, oth_far]
    out = list(mine)
    for block in mine:
        out.append(swap(block, "core"))
    return out


def pick_kernel(plan_ref, spread_ref, out_ref, sem):
    cols = spread_ref.shape[3]
    copies = []
    for k in range(4):
        owner = plan_ref[k // 2, k % 2]
        for g in range(NGRP):
            copies.append(pltpu.make_async_copy(
                spread_ref.at[g, owner], out_ref.at[k, :, pl.ds(g * cols, cols)], sem))
    for c in copies:
        c.start()
    for c in copies:
        c.wait()


def pick_owners(plan, spread):
    part, cols = spread.shape[2:]
    return pl.pallas_call(
        pick_kernel,
        out_shape=jax.ShapeDtypeStruct((4, part, NGRP * cols), spread.dtype),
        in_specs=[pl.BlockSpec(memory_space=pltpu.SMEM), pl.BlockSpec(memory_space=pl.ANY)],
        out_specs=pl.BlockSpec(memory_space=pltpu.VMEM),
        scratch_shapes=[pltpu.SemaphoreType.DMA],
        name="pick_owners",
    )(plan, spread)


def block_indices():
    yhi, x, core = (lax.axis_index(a) for a in WIDE)
    places = [(0, 0), (1, 0), (0, 3), (0, 1), (1, 3), (1, 1), (0, 2), (1, 2)]
    out = []
    for flip in (0, 1):
        for dy, dx in places:
            out.append(((yhi ^ dy) * 4 + (x + dx) % 4) * 2 + (core ^ flip))
    return jnp.stack(out).astype(jnp.int32)


def pair_kernel(*refs):
    where_ref, energy_ref, vir_ref = refs[:3]
    own_rows = refs[3:3 + NGRP]
    cuts = refs[3 + NGRP:3 + NGRP + NWIDE], refs[3 + NGRP + NWIDE:3 + NGRP + 2 * NWIDE]
    out_ref, rows_i, rows_j, amp, comb, obuf, in_sem, out_sem = refs[3 + NGRP + 2 * NWIDE:]
    virt, aux = rows_i.shape
    count = cuts[0][0].shape[0]
    wide_p = own_rows[0].shape[1]
    me = where_ref[NWIDE]
    copies = [[] for _ in range(count)]
    for g, source in enumerate(own_rows):
        start = pl.multiple_of((me ^ g) * wide_p, wide_p)
        copies[0].append(pltpu.make_async_copy(
            source, rows_i.at[:, pl.ds(start, wide_p)], in_sem.at[0]))
    for k in range(count):
        base = k * virt
        for blocks in cuts:
            part = blocks[0].shape[1]
            for b in range(NWIDE):
                start = pl.multiple_of(where_ref[b] * part, 16)
                copies[k].append(pltpu.make_async_copy(
                    blocks[b].at[k], rows_j.at[pl.ds(base + start, part), :], in_sem.at[k]))
            base += NWIDE * part
    for group in copies:
        for c in group:
            c.start()
    vrow = vir_ref[...]
    vcol = jnp.broadcast_to(vrow, (128, virt)).T[:, :1]
    tile = 256
    for k in range(count):
        for c in copies[k]:
            c.wait()
        at = k * virt
        inter = lax.dot_general(
            rows_i[...], rows_j[at:at + virt, :], (((1,), (1,)), ((), ())),
            preferred_element_type=jnp.float32)
        amp[...] = inter / ((energy_ref[0] + energy_ref[1 + k]) - vcol - vrow)
        for i in range(0, virt, tile):
            for j in range(0, virt, tile):
                comb[i:i + tile, at + j:at + j + tile] = (
                    2.0 * amp[i:i + tile, j:j + tile] - amp[j:j + tile, i:i + tile].T
                ).astype(jnp.bfloat16)
    step = obuf.shape[2]
    nstep = aux // step

    def out_copy(n):
        return pltpu.make_async_copy(
            obuf.at[n % 2], out_ref.at[:, pl.ds(n * step, step)], out_sem.at[n % 2])

    for n in range(nstep):
        total = jnp.dot(comb[...], rows_j[:, n * step:(n + 1) * step],
                        preferred_element_type=jnp.float32)
        if n >= 2:
            out_copy(n - 2).wait()
        obuf[n % 2] = total
        out_copy(n).start()
    for n in range(max(nstep - 2, 0), nstep):
        out_copy(n).wait()


def pair_terms(where, energies, vir, rows_i, first, second):
    count, _, aux = first[0].shape
    virt = rows_i[0].shape[0]
    step = 512
    anyspec = pl.BlockSpec(memory_space=pl.ANY)
    smem = pl.BlockSpec(memory_space=pltpu.SMEM)
    vmem = pl.BlockSpec(memory_space=pltpu.VMEM)
    args = [where, energies, vir, *rows_i, *first, *second]
    return pl.pallas_call(
        pair_kernel,
        out_shape=jax.ShapeDtypeStruct((virt, aux), jnp.float32),
        in_specs=[smem, smem, vmem] + [anyspec] * (len(args) - 3),
        out_specs=anyspec,
        scratch_shapes=[
            pltpu.VMEM((virt, aux), jnp.bfloat16),
            pltpu.VMEM((count * virt, aux), jnp.bfloat16),
            pltpu.VMEM((virt, virt), jnp.float32),
            pltpu.VMEM((virt, count * virt), jnp.bfloat16),
            pltpu.VMEM((2, virt, step), jnp.float32),
            pltpu.SemaphoreType.DMA((count,)),
            pltpu.SemaphoreType.DMA((2,)),
        ],
        compiler_params=pltpu.CompilerParams(vmem_limit_bytes=56 * 1024 * 1024),
        cost_estimate=pl.CostEstimate(
            flops=4 * count * virt * virt * aux, transcendentals=0,
            bytes_accessed=2 * (count + 1) * virt * aux + 4 * virt * aux),
        name="pair_terms",
    )(*args)


def shards(half_integrals, coeff_virtual, occ_energy, vir_energy, plan):
    half = half_integrals[0]
    virt = coeff_virtual.shape[1]
    cut = virt // 3
    grp = lax.axis_index(GRP)
    wide = lax.axis_index(WIDE)

    def form(coeff):
        return jnp.einsum(
            "imp,ma->iap", half, coeff, preferred_element_type=jnp.float32
        ).astype(jnp.bfloat16)

    def spread_rows(rows):
        orbs, size, cols = rows.shape
        part = size // NWIDE
        out = lax.all_to_all(rows.reshape(orbs * NWIDE, part, cols), ALL, 0, 0, tiled=True)
        return out.reshape(NGRP, NWIDE, part, cols)

    rows_a = form(coeff_virtual[:, :cut])
    spread_a = spread_rows(rows_a)
    rows_b = form(coeff_virtual[:, cut:])
    spread_b = spread_rows(rows_b)
    rows = jnp.concatenate([rows_a, rows_b], axis=1)
    rows_i = []
    for s in range(NGRP):
        piece = lax.dynamic_index_in_dim(rows, grp ^ s, 0, keepdims=False)
        if s:
            piece = lax.ppermute(piece, GRP, [(g, g ^ s) for g in range(NGRP)])
        rows_i.append(piece)
    energy = lax.dynamic_slice_in_dim(occ_energy, grp, 1, 1)[:, 0]
    my_energy = lax.dynamic_slice_in_dim(energy, wide, 1)
    e_own = jnp.take(energy, plan.reshape(-1), axis=0)
    small = (jnp.concatenate([block_indices(), grp[None].astype(jnp.int32)]),
             jnp.concatenate([my_energy, e_own]), vir_energy[None, :])
    spread_b, (where, energies, vrow) = lax.optimization_barrier((spread_b, small))
    first = gather_wide(pick_owners(plan, spread_a))
    second = gather_wide(pick_owners(plan, spread_b))
    density = pair_terms(where, energies, vrow, rows_i, first, second)
    return density[None, None]


def solution(mesh):
    fine = Mesh(mesh.devices.reshape(2, 4, 2, 4, 2), GRP + WIDE)
    return jax.shard_map(
        shards,
        mesh=fine,
        in_specs=(P(WIDE, None, None, GRP), P(), P(), P(), P()),
        out_specs=P(WIDE, GRP, None, None),
        check_vma=False,
    )
```
